32 devices in a mesh: seq: 4 (over y, x), tp: 8 (over z, core).
Axes of the slice: x: 2, y: 2, z: 4, core: 2. Of those that a mesh axis runs over, the one named last changes fastest.
Arguments:
- tokens: bfloat16 [1, 512, 4096], P(None, 'seq', 'tp'), may hold values from -6 to 6
- projections: bfloat16 [4096, 3, 4096], P(None, None, 'tp'), may hold values from -1.5 to 1.5
- out_weight: bfloat16 [4096, 4096], P('tp'), may hold values from -0.09375 to 0.09375
- gain_in: float32 [4096], P('tp'), may hold values from 0.5 to 1.5
- gain_out: float32 [4096], P('tp'), may hold values from 0.5 to 1.5
- iterates: float32 [5, 1, 512, 4096], P(None, None, 'seq', 'tp'), may hold values from -5 to 5
- images: float32 [5, 1, 512, 4096], P(None, None, 'seq', 'tp'), may hold values from -330 to 330
Outputs:
- mixed: float32 [1, 512, 4096], P(None, 'seq', 'tp')
- image: float32 [1, 512, 4096], P(None, 'seq', 'tp')
The draws below stay inside these ranges and needn't reach their ends.
All inputs are finite; a program needn't handle non-finite values.
Results may differ from the reference program's by a relative error of at most 0.013.
Values may be sent and summed in bfloat16 or wider, within the bound.
No kernel may reach another device: no remote copies, remote signals or barrier semaphores. Data moves between devices by JAX's collectives and lax.ppermute only.
A program may use at most 64 MiB of HBM per device.

```python
import jax
import jax.numpy as jnp
from jax import lax

D = 4096
H = 32
HEAD_SIZE = 128
MEM = 5
ITERS = 2
BATCH = 1
SEQ = 512


scale_blocks = 16


def draw_projections(key, part):
    first_key = jax.random.fold_in(key, 0)
    base = jnp.clip(jax.random.normal(first_key, (D, 3, H * HEAD_SIZE), jnp.float32), -6.0, 6.0) * D ** (-0.5)
    return jnp.clip(base, -1.5, 1.5).astype(jnp.bfloat16)


def history_parts(key):
    inner = jax.random.fold_in(key, 7)
    token_key, base_key, common_key, noise_key, mixing_key, block_key = jax.random.split(inner, 6)
    field_shape = (BATCH, SEQ, D)
    shape = (MEM, BATCH, SEQ, D)
    token_part = jnp.clip(jax.random.normal(token_key, field_shape, jnp.float32), -6.0, 6.0)
    base = jnp.clip(jax.random.normal(base_key, shape, jnp.float32), -5.0, 5.0)
    common = jnp.clip(jax.random.normal(common_key, (3,) + field_shape, jnp.float32), -5.0, 5.0)
    noise_weight = 0.5
    noise = jnp.clip(jax.random.normal(noise_key, shape, jnp.float32), -5.0, 5.0)
    components = jnp.concatenate([token_part[None], common], axis=0)
    mixing = jnp.clip(0.5 * jax.random.normal(mixing_key, (MEM, 4), jnp.float32), -1.0, 1.0)
    shared = jnp.einsum('mk,kbsd->mbsd', mixing, components, precision=lax.Precision.HIGHEST)
    scale_table = jnp.exp(jax.random.uniform(block_key, (MEM, scale_blocks, scale_blocks), jnp.float32, -1.5, 1.5))
    seq_block = jnp.arange(SEQ, dtype=jnp.int32) * scale_blocks // SEQ
    feature_block = jnp.arange(D, dtype=jnp.int32) * scale_blocks // D
    block_scale = scale_table[:, seq_block, :][:, :, feature_block]
    level = 0.25 * 2.0 ** ((MEM - 1 - jnp.arange(MEM).astype(jnp.float32)) / 2.0)
    ramp = 1.0 + 2.0 * jnp.arange(SEQ).astype(jnp.float32) / max(SEQ - 1, 1)
    weighting = level[:, None, None] * ramp[None, :, None] * block_scale
    residual = (shared + noise_weight * noise) * weighting[:, None]
    return (token_part, base, base + residual)


def draw_tokens(key, part):
    return history_parts(key)[0].astype(jnp.bfloat16)


def draw_iterates(key, part):
    return history_parts(key)[1]


def draw_images(key, part):
    return history_parts(key)[2]


def levels(rng, shape, shards, smallest, high):
    loudness = 1.0
    for dim, blocks in shards:
        heights = jax.random.uniform(jax.random.fold_in(jax.random.fold_in(rng, 6), dim), (blocks,), jnp.float32, smallest / len(shards), high / len(shards))
        loudness = loudness * jnp.repeat(jnp.exp(heights), shape[dim] // blocks).reshape((-1,) + (1,) * (len(shape) - 1 - dim))
    return loudness


def scatter_about(stream_key, shape, deviation, reach, cuts=(), kind=jnp.bfloat16):
    gain = levels(stream_key, shape, cuts, -0.22, 0.18) if cuts else 1.0
    drawn = jax.random.normal(stream_key, shape, jnp.float32) * deviation * gain
    return jnp.minimum(jnp.maximum(drawn, -reach), reach).astype(kind)


def setup_inputs(seed: int = 0) -> dict:
    key_of = jax.random.split(jax.random.key(seed), 8)
    return {
        "tokens": draw_tokens(jax.random.fold_in(key_of[7], 71), 0),
        "projections": draw_projections(jax.random.fold_in(key_of[7], 71), 0),
        "out_weight": scatter_about(key_of[2], (H * HEAD_SIZE, D), (H * HEAD_SIZE) ** -0.5, 0.09375, ((0, 8),)),
        "gain_in": jnp.clip(1.0 + 0.1 * jax.random.normal(key_of[3], (D,), jnp.float32), 0.5, 1.5),
        "gain_out": jnp.clip(1.0 + 0.1 * jax.random.normal(key_of[4], (D,), jnp.float32), 0.5, 1.5),
        "iterates": draw_iterates(jax.random.fold_in(key_of[7], 71), 0),
        "images": draw_images(jax.random.fold_in(key_of[7], 71), 0),
    }


epsilon = 1e-05
rope_base = 10000.0
ridge_factor = 0.01

def inverse_rms(value_rows):
    return lax.rsqrt(lax.optimization_barrier(jnp.mean(value_rows * value_rows, axis=-1, keepdims=True)) + epsilon)

def rotate(vectors, positions):
    half_dim = vectors.shape[-1] // 2
    frequency = rope_base ** (-2.0 * jnp.arange(half_dim).astype(jnp.float32) / vectors.shape[-1])
    angles = positions[:, None] * frequency[None, :]
    cosine = jnp.cos(angles)
    sine_part = jnp.sin(angles)
    first_half = vectors[..., :half_dim]
    second_half = vectors[..., half_dim:]
    return jnp.concatenate([first_half * cosine - second_half * sine_part, second_half * cosine + first_half * sine_part], axis=-1)

def solve_small(matrix, target):
    extent = matrix.shape[0]
    indices = jnp.arange(extent)
    for column in range(extent):
        factor = jnp.where(indices > column, matrix[:, column] / matrix[column, column], 0.0)
        matrix = matrix - factor[:, None] * matrix[column][None, :]
        target = target - factor * target[column]
    answer = jnp.zeros_like(target)
    for column in reversed(range(extent)):
        entry_value = (target[column] - jnp.sum(matrix[column] * answer)) / matrix[column, column]
        answer = answer.at[column].set(entry_value)
    return answer

def anderson_weights(gram):
    extent = gram.shape[0]
    ridge = ridge_factor * jnp.trace(gram) / extent
    regular = gram + ridge * jnp.eye(extent, dtype=gram.dtype)
    solved = solve_small(regular, jnp.ones((extent,), gram.dtype))
    return solved / jnp.sum(solved)

def attend_head(operands):
    query_rows, key_rows, value_rows = operands
    length = query_rows.shape[1]
    logit_scores = jnp.einsum('oir,osr->ois', query_rows.astype(jnp.float32), key_rows.astype(jnp.float32), precision=lax.Precision.HIGHEST) * HEAD_SIZE ** (-0.5)
    causal = jnp.arange(length)[None, :] <= jnp.arange(length)[:, None]
    logit_scores = jnp.where(causal[None], logit_scores, -1e+30)
    highest = lax.optimization_barrier(jnp.max(logit_scores, axis=-1, keepdims=True))
    softmax_weights = jnp.where(causal[None], jnp.exp(logit_scores - highest), 0.0)
    total = lax.optimization_barrier(jnp.sum(softmax_weights, axis=-1, keepdims=True))
    value_mixture = jnp.einsum('atf,afv->atv', softmax_weights.astype(jnp.bfloat16).astype(jnp.float32), value_rows.astype(jnp.float32), precision=lax.Precision.HIGHEST)
    return (value_mixture / total).astype(jnp.bfloat16)

def layer_map(field, tokens, projections, out_weight, gain_in, gain_out):
    batch_count, length, width = field.shape
    heads = projections.shape[2] // HEAD_SIZE
    normed = (field * inverse_rms(field) * gain_in).astype(jnp.bfloat16)
    mapped = jnp.einsum('bsd,dce->bsce', normed.astype(jnp.float32), projections.astype(jnp.float32), precision=lax.Precision.HIGHEST)
    pieces = mapped.reshape(batch_count, length, 3, heads, HEAD_SIZE).transpose(2, 3, 0, 1, 4)
    positions = jnp.arange(length).astype(jnp.float32)
    query_rows = rotate(pieces[0], positions).astype(jnp.bfloat16)
    key_rows = rotate(pieces[1], positions).astype(jnp.bfloat16)
    value_rows = pieces[2].astype(jnp.bfloat16)
    outputs = lax.map(attend_head, (query_rows, key_rows, value_rows))
    joined = outputs.transpose(1, 2, 0, 3).reshape(batch_count * length, heads * HEAD_SIZE)
    attention = jnp.dot(joined, out_weight, preferred_element_type=jnp.float32).reshape(batch_count, length, width)
    summed = tokens.astype(jnp.float32) + attention
    return summed * inverse_rms(summed) * gain_out

def reference(tokens, projections, out_weight, gain_in, gain_out, iterates, images):
    mixed = iterates[0]
    image = images[0]
    for step_index in range(ITERS):
        residuals = images - iterates
        gram = jnp.einsum('mbsd,nbsd->mn', residuals, residuals, precision=lax.Precision.HIGHEST)
        alpha = anderson_weights(gram)
        mixed = jnp.einsum('m,mbsd->bsd', alpha, images, precision=lax.Precision.HIGHEST)
        image = layer_map(mixed, tokens, projections, out_weight, gain_in, gain_out)
        iterates = jnp.concatenate([iterates[1:], mixed[None]], axis=0)
        images = jnp.concatenate([images[1:], image[None]], axis=0)
    return (mixed, image)
```

```python
import jax
import jax.numpy as jnp
from jax import lax
from jax.experimental import pallas as pl
from jax.experimental.pallas import tpu as pltpu
from jax.sharding import PartitionSpec as P

HEAD_SIZE = 128
ITERS = 2
LANES = 128


epsilon = 1e-05
rope_base = 10000.0
ridge_factor = 0.01


def pair_list(extent):
    return [(m, n) for m in range(extent) for n in range(m, extent)]


def gram_kernel(images_ref, iterates_ref, out_ref):
    extent, length, width = images_ref.shape
    pairs = pair_list(extent)
    rows = 8

    def step(index, sums):
        place = pl.ds(pl.multiple_of(index * rows, rows), rows)
        residuals = [images_ref[m, place, :] - iterates_ref[m, place, :] for m in range(extent)]
        grown = []
        for total, (m, n) in zip(sums, pairs):
            product = residuals[m] * residuals[n]
            for lane in range(0, width, LANES):
                total = total + product[:, lane:lane + LANES]
            grown.append(total)
        return tuple(grown)

    zero = jnp.zeros((rows, LANES), jnp.float32)
    sums = lax.fori_loop(0, length // rows, step, tuple(zero for _ in pairs))
    for place, total in enumerate(sums):
        out_ref[place:place + 1, :] = jnp.sum(total, axis=0, keepdims=True)


def gram_partials(images, iterates):
    count = len(pair_list(images.shape[0]))
    return pl.pallas_call(
        gram_kernel,
        out_shape=jax.ShapeDtypeStruct((count, LANES), jnp.float32),
    )(images, iterates)


def solve_kernel(extent, rows_ref, out_ref):
    table = {}
    for place, (m, n) in enumerate(pair_list(extent)):
        value = jnp.sum(rows_ref[place:place + 1, :], axis=1, keepdims=True)
        value = jnp.broadcast_to(value, (1, LANES))
        table[m, n] = value
        table[n, m] = value
    trace = table[0, 0]
    for m in range(1, extent):
        trace = trace + table[m, m]
    ridge = ridge_factor * trace / extent
    for m in range(extent):
        table[m, m] = table[m, m] + ridge
    target = [jnp.ones((1, LANES), jnp.float32) for _ in range(extent)]
    for column in range(extent):
        for row in range(column + 1, extent):
            factor = table[row, column] / table[column, column]
            for other in range(column + 1, extent):
                table[row, other] = table[row, other] - factor * table[column, other]
            target[row] = target[row] - factor * target[column]
    answer = [None] * extent
    for column in reversed(range(extent)):
        value = target[column]
        for other in range(column + 1, extent):
            value = value - table[column, other] * answer[other]
        answer[column] = value / table[column, column]
    total = answer[0]
    for m in range(1, extent):
        total = total + answer[m]
    for m in range(extent):
        out_ref[m:m + 1, :] = answer[m] / total


def anderson_weights(rows, extent):
    def body(rows_ref, out_ref):
        solve_kernel(extent, rows_ref, out_ref)

    return pl.pallas_call(
        body, out_shape=jax.ShapeDtypeStruct((extent, LANES), jnp.float32)
    )(rows)[:, 0]


def project_kernel(full_width, order_ref, x_ref, w_ref, gain_ref, cos_ref, sin_ref, out_ref, acc, squares):
    step = pl.program_id(0)

    @pl.when(step == 0)
    def _():
        acc[...] = jnp.zeros_like(acc)
        squares[...] = jnp.zeros_like(squares)

    block = x_ref[0]
    for part in range(3):
        acc[part] += jnp.dot(block, w_ref[part], preferred_element_type=jnp.float32)
    plain = block.astype(jnp.float32) / gain_ref[0]
    squares[...] += jnp.sum(plain * plain, axis=1, keepdims=True)

    @pl.when(step == pl.num_programs(0) - 1)
    def _():
        scale = lax.rsqrt(squares[...] / full_width + epsilon)
        half = HEAD_SIZE // 2
        cosine = cos_ref[...]
        sine = sin_ref[...]
        for part in range(3):
            for head in range(0, acc.shape[2], HEAD_SIZE):
                value = acc[part, :, head:head + HEAD_SIZE] * scale
                if part < 2:
                    swapped = jnp.concatenate([value[:, half:], value[:, :half]], axis=1)
                    value = value * cosine + swapped * sine
                out_ref[part, :, head:head + HEAD_SIZE] = value.astype(jnp.bfloat16)


def project(order, gathered, weights, gains, cosine, sine):
    count, length, depth = gathered.shape
    width = weights.shape[2]
    def body(*refs):
        project_kernel(count * depth, *refs)

    return pl.pallas_call(
        body,
        grid_spec=pltpu.PrefetchScalarGridSpec(
            num_scalar_prefetch=1,
            grid=(count,),
            in_specs=[
                pl.BlockSpec((1, length, depth), lambda k, order: (k, 0, 0)),
                pl.BlockSpec((3, depth, width), lambda k, order: (0, order[k], 0)),
                pl.BlockSpec((1, 1, depth), lambda k, order: (order[k], 0, 0)),
                pl.BlockSpec((length, HEAD_SIZE), lambda k, order: (0, 0)),
                pl.BlockSpec((length, HEAD_SIZE), lambda k, order: (0, 0)),
            ],
            out_specs=pl.BlockSpec((3, length, width), lambda k, order: (0, 0, 0)),
            scratch_shapes=[
                pltpu.VMEM((3, length, width), jnp.float32),
                pltpu.VMEM((length, 1), jnp.float32),
            ],
        ),
        out_shape=jax.ShapeDtypeStruct((3, length, width), jnp.bfloat16),
        cost_estimate=pl.CostEstimate(
            flops=2 * length * count * depth * 3 * width,
            bytes_accessed=2 * count * depth * 3 * width,
            transcendentals=0,
        ),
    )(order, gathered, weights, gains, cosine, sine)


def exchange(value, axes):
    count = lax.axis_size(axes)
    spread = jnp.broadcast_to(value[None], (count,) + value.shape)
    return lax.all_to_all(spread, axes, 0, 0)


def swap_cores(value):
    return lax.ppermute(value, "tp", [(i, i ^ 1) for i in range(lax.axis_size("tp"))])


def from_chip(value, ahead):
    count = lax.axis_size("tp")
    chips = count // 2
    pairs = [(i, ((i // 2 - ahead) % chips) * 2 + i % 2) for i in range(count)]
    return lax.ppermute(value, "tp", pairs)


def gather_features(value):
    chips = lax.axis_size("tp") // 2
    same = [value] + [from_chip(value, ahead) for ahead in range(1, chips)]
    blocks = []
    for block in same:
        blocks += [block, swap_cores(block)]
    return jnp.stack(blocks)


def scatter_sum(partial, chip, core):
    count = lax.axis_size("tp")
    chips = count // 2
    width = partial.shape[1] // count

    def piece(ahead, which):
        start = (((chip + ahead) % chips) * 2 + which) * width
        return lax.dynamic_slice_in_dim(partial, start, width, axis=1)

    total = None
    for ahead in list(range(1, chips)) + [0]:
        other = swap_cores(piece(ahead, 1 - core).astype(jnp.bfloat16))
        pair_sum = piece(ahead, core).astype(jnp.float32) + other.astype(jnp.float32)
        if ahead:
            pair_sum = from_chip(pair_sum.astype(jnp.bfloat16), chips - ahead).astype(jnp.float32)
        total = pair_sum if total is None else total + pair_sum
    return total


def shards(tokens, projections, out_weight, gain_in, gain_out, iterates, images):
    tokens = tokens[0].astype(jnp.float32)
    iterates = iterates[:, 0]
    images = images[:, 0]
    extent, length, width = images.shape
    tp_count = lax.axis_size("tp")
    seq_count = lax.axis_size("seq")
    full_width = width * tp_count
    tp_index = lax.axis_index("tp")
    seq_index = lax.axis_index("seq")
    chip, core = tp_index // 2, tp_index % 2
    heads = projections.shape[2] // HEAD_SIZE
    weights = projections.transpose(1, 0, 2)
    query_index = seq_index * length + jnp.arange(length, dtype=jnp.int32)
    half = HEAD_SIZE // 2
    frequency = rope_base ** (-2.0 * jnp.arange(half).astype(jnp.float32) / HEAD_SIZE)
    angles = query_index.astype(jnp.float32)[:, None] * frequency[None, :]
    cosine = jnp.cos(angles)
    sine = jnp.sin(angles)
    cosine = jnp.concatenate([cosine, cosine], axis=1)
    sine = jnp.concatenate([-sine, sine], axis=1)
    order = jnp.stack(
        [
            ((chip + ahead) % (tp_count // 2)) * 2 + (core + j) % 2
            for ahead in range(tp_count // 2)
            for j in range(2)
        ]
    ).astype(jnp.int32)
    pairs = pair_list(extent)
    payload = jnp.concatenate([gram_partials(images, iterates), gain_in.reshape(-1, LANES)], axis=0)
    received = exchange(payload, ("seq", "tp"))
    gram_rows = jnp.sum(received[:, :len(pairs)], axis=0)
    full_gain = received[:tp_count, len(pairs):].reshape(tp_count, 1, width)
    offsets = [shift for shift in range(seq_count)]
    key_index = jnp.concatenate(
        [(seq_index ^ shift) * length + jnp.arange(length, dtype=jnp.int32) for shift in offsets]
    )
    allowed = (key_index[None, :] <= query_index[:, None])[None]
    score_scale = HEAD_SIZE ** (-0.5)
    mixed = image = None
    kept = None
    for step_index in range(ITERS):
        alpha = anderson_weights(gram_rows, extent)
        mixed = sum(alpha[m] * images[m] for m in range(extent))
        scaled_input = (mixed * gain_in).astype(jnp.bfloat16)
        gathered = gather_features(scaled_input)
        parts = project(order, gathered, weights, full_gain, cosine, sine)
        own = parts[1:]
        blocks = [own] + [
            lax.ppermute(own, "seq", [(i, i ^ shift) for i in range(seq_count) if i < i ^ shift])
            for shift in offsets[1:]
        ]
        both = jnp.concatenate(blocks, axis=1).reshape(2, seq_count * length, heads, HEAD_SIZE)
        query_rows = parts[0].reshape(length, heads, HEAD_SIZE)
        scores = jnp.einsum(
            "qhd,khd->hqk", query_rows, both[0], preferred_element_type=jnp.float32
        ) * score_scale
        scores = jnp.where(allowed, scores, -1e30)
        best = jnp.max(scores, axis=-1, keepdims=True)
        softmax_weights = jnp.where(allowed, jnp.exp(scores - best), 0.0)
        total = jnp.sum(softmax_weights, axis=-1)
        accum = jnp.einsum(
            "hqk,khd->hqd",
            softmax_weights.astype(jnp.bfloat16),
            both[1],
            preferred_element_type=jnp.float32,
        )
        attended = (accum / total[..., None]).astype(jnp.bfloat16)
        attended = attended.transpose(1, 0, 2).reshape(length, heads * HEAD_SIZE)
        partial = jnp.dot(attended, out_weight, preferred_element_type=jnp.float32)
        summed = tokens + scatter_sum(partial.astype(jnp.bfloat16), chip, core)
        scaled = summed * gain_out
        squares = jnp.sum(summed * summed, axis=-1)
        if step_index + 1 == ITERS:
            squares = jnp.sum(exchange(squares[None], "tp"), axis=(0, 1))
            image = scaled * lax.rsqrt(squares / full_width + epsilon)[:, None]
        else:
            residuals = kept if kept is not None else images - iterates
            kept = residuals[1:]
            stats = [squares]
            stats += [jnp.sum(scaled * kept[m], axis=-1) for m in range(extent - 1)]
            stats += [jnp.sum(scaled * scaled, axis=-1), jnp.sum(scaled * mixed, axis=-1)]
            stats += [jnp.sum(mixed * kept[m], axis=-1) for m in range(extent - 1)]
            stats += [jnp.sum(mixed * mixed, axis=-1)]
            received = exchange(jnp.stack(stats), ("seq", "tp"))
            sums = jnp.sum(received.reshape((seq_count, tp_count) + received.shape[1:]), axis=1)
            row_scale = lax.rsqrt(sums[:, 0] / full_width + epsilon)
            cross = sums[:, 1:extent] * row_scale[:, None] - sums[:, extent + 2:2 * extent + 1]
            cross = jnp.sum(cross, axis=0)
            own_terms = jnp.sum(
                row_scale * row_scale * sums[:, extent]
                - 2.0 * row_scale * sums[:, extent + 1]
                + sums[:, 2 * extent + 1],
                axis=0,
            )
            fresh = []
            for m, n in pairs:
                if n < extent - 1:
                    fresh.append(gram_rows[pairs.index((m + 1, n + 1))])
                elif m < extent - 1:
                    fresh.append(cross[m])
                else:
                    fresh.append(own_terms)
            gram_rows = jnp.stack(fresh)
            own_scale = lax.dynamic_index_in_dim(row_scale, seq_index, 0, keepdims=False)
            image = scaled * own_scale[:, None]
            kept = jnp.concatenate([kept, (image - mixed)[None]], axis=0)
            images = jnp.concatenate([images[1:], image[None]], axis=0)
    return (mixed[None], image[None])


def solution(mesh):
    in_specs = (
        P(None, "seq", "tp"),
        P(None, None, "tp"),
        P("tp", None),
        P("tp"),
        P("tp"),
        P(None, None, "seq", "tp"),
        P(None, None, "seq", "tp"),
    )
    out_specs = (P(None, "seq", "tp"), P(None, "seq", "tp"))
    return jax.shard_map(shards, mesh=mesh, in_specs=in_specs, out_specs=out_specs, check_vma=False)
```

```python
import jax
import jax.numpy as jnp
from jax import lax
from jax.experimental import pallas as pl
from jax.experimental.pallas import tpu as pltpu
from jax.sharding import PartitionSpec as P

HEAD_SIZE = 128
ITERS = 2
LANES = 128


epsilon = 1e-05
rope_base = 10000.0
ridge_factor = 0.01


def pair_list(extent):
    return [(m, n) for m in range(extent) for n in range(m, extent)]


def gram_kernel(images_ref, iterates_ref, out_ref):
    extent, length, width = images_ref.shape
    pairs = pair_list(extent)
    rows = 8

    def step(index, sums):
        place = pl.ds(pl.multiple_of(index * rows, rows), rows)
        residuals = [images_ref[m, place, :] - iterates_ref[m, place, :] for m in range(extent)]
        grown = []
        for total, (m, n) in zip(sums, pairs):
            product = residuals[m] * residuals[n]
            for lane in range(0, width, LANES):
                total = total + product[:, lane:lane + LANES]
            grown.append(total)
        return tuple(grown)

    zero = jnp.zeros((rows, LANES), jnp.float32)
    sums = lax.fori_loop(0, length // rows, step, tuple(zero for _ in pairs))
    for place, total in enumerate(sums):
        out_ref[place:place + 1, :] = jnp.sum(total, axis=0, keepdims=True)


def gram_partials(images, iterates):
    count = len(pair_list(images.shape[0]))
    return pl.pallas_call(
        gram_kernel,
        out_shape=jax.ShapeDtypeStruct((count, LANES), jnp.float32),
    )(images, iterates)


def solve_kernel(extent, rows_ref, out_ref):
    table = {}
    for place, (m, n) in enumerate(pair_list(extent)):
        value = jnp.sum(rows_ref[place:place + 1, :], axis=1, keepdims=True)
        value = jnp.broadcast_to(value, (1, LANES))
        table[m, n] = value
        table[n, m] = value
    trace = table[0, 0]
    for m in range(1, extent):
        trace = trace + table[m, m]
    ridge = ridge_factor * trace / extent
    for m in range(extent):
        table[m, m] = table[m, m] + ridge
    target = [jnp.ones((1, LANES), jnp.float32) for _ in range(extent)]
    for column in range(extent):
        for row in range(column + 1, extent):
            factor = table[row, column] / table[column, column]
            for other in range(column + 1, extent):
                table[row, other] = table[row, other] - factor * table[column, other]
            target[row] = target[row] - factor * target[column]
    answer = [None] * extent
    for column in reversed(range(extent)):
        value = target[column]
        for other in range(column + 1, extent):
            value = value - table[column, other] * answer[other]
        answer[column] = value / table[column, column]
    total = answer[0]
    for m in range(1, extent):
        total = total + answer[m]
    for m in range(extent):
        out_ref[m:m + 1, :] = answer[m] / total


def anderson_weights(rows, extent):
    def body(rows_ref, out_ref):
        solve_kernel(extent, rows_ref, out_ref)

    return pl.pallas_call(
        body, out_shape=jax.ShapeDtypeStruct((extent, LANES), jnp.float32)
    )(rows)[:, 0]


def project_kernel(full_width, order_ref, x_ref, w_ref, gain_ref, cos_ref, sin_ref, out_ref, acc, squares):
    step = pl.program_id(0)

    @pl.when(step == 0)
    def _():
        acc[...] = jnp.zeros_like(acc)
        squares[...] = jnp.zeros_like(squares)

    block = x_ref[0]
    for part in range(3):
        acc[part] += jnp.dot(block, w_ref[part], preferred_element_type=jnp.float32)
    plain = block.astype(jnp.float32) / gain_ref[0]
    squares[...] += jnp.sum(plain * plain, axis=1, keepdims=True)

    @pl.when(step == pl.num_programs(0) - 1)
    def _():
        scale = lax.rsqrt(squares[...] / full_width + epsilon)
        half = HEAD_SIZE // 2
        cosine = cos_ref[...]
        sine = sin_ref[...]
        for part in range(3):
            for head in range(0, acc.shape[2], HEAD_SIZE):
                value = acc[part, :, head:head + HEAD_SIZE] * scale
                if part < 2:
                    swapped = jnp.concatenate([value[:, half:], value[:, :half]], axis=1)
                    value = value * cosine + swapped * sine
                out_ref[part, :, head:head + HEAD_SIZE] = value.astype(jnp.bfloat16)


def project(order, gathered, weights, gains, cosine, sine):
    count, length, depth = gathered.shape
    width = weights.shape[2]
    def body(*refs):
        project_kernel(count * depth, *refs)

    return pl.pallas_call(
        body,
        grid_spec=pltpu.PrefetchScalarGridSpec(
            num_scalar_prefetch=1,
            grid=(count,),
            in_specs=[
                pl.BlockSpec((1, length, depth), lambda k, order: (k, 0, 0)),
                pl.BlockSpec((3, depth, width), lambda k, order: (0, order[k], 0)),
                pl.BlockSpec((1, 1, depth), lambda k, order: (order[k], 0, 0)),
                pl.BlockSpec((length, HEAD_SIZE), lambda k, order: (0, 0)),
                pl.BlockSpec((length, HEAD_SIZE), lambda k, order: (0, 0)),
            ],
            out_specs=pl.BlockSpec((3, length, width), lambda k, order: (0, 0, 0)),
            scratch_shapes=[
                pltpu.VMEM((3, length, width), jnp.float32),
                pltpu.VMEM((length, 1), jnp.float32),
            ],
        ),
        out_shape=jax.ShapeDtypeStruct((3, length, width), jnp.bfloat16),
        cost_estimate=pl.CostEstimate(
            flops=2 * length * count * depth * 3 * width,
            bytes_accessed=2 * count * depth * 3 * width,
            transcendentals=0,
        ),
    )(order, gathered, weights, gains, cosine, sine)


def attend_kernel(shifts, order_ref, parts_ref, *refs):
    received = refs[:shifts]
    weight_ref, out_ref, attended = refs[shifts:]
    length, width = attended.shape
    count = pl.num_programs(0)

    @pl.when(pl.program_id(0) == 0)
    def _():
        rows = lax.broadcasted_iota(jnp.int32, (length, length), 0)
        columns = lax.broadcasted_iota(jnp.int32, (length, length), 1)
        allowed = [columns <= rows]
        for shift in range(shifts):
            allowed.append(jnp.full((length, length), order_ref[count + shift], jnp.int32) > 0)
        for head in range(0, width, HEAD_SIZE):
            place = slice(head, head + HEAD_SIZE)
            query = parts_ref[0, :, place]
            keys = [parts_ref[1, :, place]] + [ref[0, :, place] for ref in received]
            values = [parts_ref[2, :, place]] + [ref[1, :, place] for ref in received]
            scores = []
            for key, mask in zip(keys, allowed):
                product = lax.dot_general(
                    query, key, (((1,), (1,)), ((), ())), preferred_element_type=jnp.float32
                )
                scores.append(jnp.where(mask, product * HEAD_SIZE ** (-0.5), -1e30))
            best = scores[0]
            for score in scores[1:]:
                best = jnp.maximum(best, score)
            best = jnp.max(best, axis=1, keepdims=True)
            weights = [jnp.exp(score - best) for score in scores]
            total = weights[0]
            for weight in weights[1:]:
                total = total + weight
            total = jnp.sum(total, axis=1, keepdims=True)
            mixture = jnp.zeros((length, HEAD_SIZE), jnp.float32)
            for weight, value in zip(weights, values):
                mixture += jnp.dot(
                    weight.astype(jnp.bfloat16), value, preferred_element_type=jnp.float32
                )
            attended[:, place] = (mixture / total).astype(jnp.bfloat16)

    product = jnp.dot(attended[...], weight_ref[...], preferred_element_type=jnp.float32)
    out_ref[0] = product.astype(jnp.bfloat16)


def attend(order, parts, received, out_weight, count):
    _, length, width = parts.shape
    piece = out_weight.shape[1] // count

    def body(*refs):
        attend_kernel(len(received), *refs)

    whole = lambda k, order: (0, 0, 0)
    return pl.pallas_call(
        body,
        grid_spec=pltpu.PrefetchScalarGridSpec(
            num_scalar_prefetch=1,
            grid=(count,),
            in_specs=[pl.BlockSpec((3, length, width), whole)]
            + [pl.BlockSpec((2, length, width), whole) for _ in received]
            + [pl.BlockSpec((width, piece), lambda k, order: (0, order[k]))],
            out_specs=pl.BlockSpec((1, length, piece), lambda k, order: (k, 0, 0)),
            scratch_shapes=[pltpu.VMEM((length, width), jnp.bfloat16)],
        ),
        out_shape=jax.ShapeDtypeStruct((count, length, piece), jnp.bfloat16),
        cost_estimate=pl.CostEstimate(
            flops=2 * length * width * out_weight.shape[1],
            bytes_accessed=2 * width * out_weight.shape[1],
            transcendentals=0,
        ),
    )(order, parts, *received, out_weight)


def exchange(value, axes):
    count = lax.axis_size(axes)
    spread = jnp.broadcast_to(value[None], (count,) + value.shape)
    return lax.all_to_all(spread, axes, 0, 0)


def swap_cores(value):
    return lax.ppermute(value, "tp", [(i, i ^ 1) for i in range(lax.axis_size("tp"))])


def from_chip(value, ahead):
    count = lax.axis_size("tp")
    chips = count // 2
    pairs = [(i, ((i // 2 - ahead) % chips) * 2 + i % 2) for i in range(count)]
    return lax.ppermute(value, "tp", pairs)


def gather_features(value):
    chips = lax.axis_size("tp") // 2
    same = [value] + [from_chip(value, ahead) for ahead in range(1, chips)]
    blocks = []
    for block in same:
        blocks += [block, swap_cores(block)]
    return jnp.stack(blocks)


def scatter_sum(pieces):
    chips = lax.axis_size("tp") // 2
    total = None
    for ahead in list(range(1, chips)) + [0]:
        other = swap_cores(pieces[2 * ahead + 1])
        pair_sum = pieces[2 * ahead].astype(jnp.float32) + other.astype(jnp.float32)
        if ahead:
            pair_sum = from_chip(pair_sum.astype(jnp.bfloat16), chips - ahead).astype(jnp.float32)
        total = pair_sum if total is None else total + pair_sum
    return total


def shards(tokens, projections, out_weight, gain_in, gain_out, iterates, images):
    tokens = tokens[0].astype(jnp.float32)
    iterates = iterates[:, 0]
    images = images[:, 0]
    extent, length, width = images.shape
    tp_count = lax.axis_size("tp")
    seq_count = lax.axis_size("seq")
    full_width = width * tp_count
    tp_index = lax.axis_index("tp")
    seq_index = lax.axis_index("seq")
    chip, core = tp_index // 2, tp_index % 2
    weights = projections.transpose(1, 0, 2)
    query_index = seq_index * length + jnp.arange(length, dtype=jnp.int32)
    half = HEAD_SIZE // 2
    frequency = rope_base ** (-2.0 * jnp.arange(half).astype(jnp.float32) / HEAD_SIZE)
    angles = query_index.astype(jnp.float32)[:, None] * frequency[None, :]
    cosine = jnp.cos(angles)
    sine = jnp.sin(angles)
    cosine = jnp.concatenate([cosine, cosine], axis=1)
    sine = jnp.concatenate([-sine, sine], axis=1)
    order = jnp.stack(
        [
            ((chip + ahead) % (tp_count // 2)) * 2 + (core + j) % 2
            for ahead in range(tp_count // 2)
            for j in range(2)
        ]
    ).astype(jnp.int32)
    pairs = pair_list(extent)
    payload = jnp.concatenate([gram_partials(images, iterates), gain_in.reshape(-1, LANES)], axis=0)
    received = exchange(payload, ("seq", "tp"))
    gram_rows = jnp.sum(received[:, :len(pairs)], axis=0)
    full_gain = received[:tp_count, len(pairs):].reshape(tp_count, 1, width)
    earlier = jnp.stack([(seq_index ^ shift) < seq_index for shift in range(1, seq_count)])
    attend_order = jnp.concatenate([order, earlier.astype(jnp.int32)])
    mixed = image = None
    kept = None
    for step_index in range(ITERS):
        alpha = anderson_weights(gram_rows, extent)
        mixed = sum(alpha[m] * images[m] for m in range(extent))
        scaled_input = (mixed * gain_in).astype(jnp.bfloat16)
        gathered = gather_features(scaled_input)
        parts = project(order, gathered, weights, full_gain, cosine, sine)
        own = parts[1:]
        blocks = [
            lax.ppermute(own, "seq", [(i, i ^ shift) for i in range(seq_count) if i < i ^ shift])
            for shift in range(1, seq_count)
        ]
        pieces = attend(attend_order, parts, blocks, out_weight, tp_count)
        summed = tokens + scatter_sum(pieces)
        scaled = summed * gain_out
        squares = jnp.sum(summed * summed, axis=-1)
        if step_index + 1 == ITERS:
            squares = jnp.sum(exchange(squares[None], "tp"), axis=(0, 1))
            image = scaled * lax.rsqrt(squares / full_width + epsilon)[:, None]
        else:
            residuals = kept if kept is not None else images - iterates
            kept = residuals[1:]
            stats = [squares]
            stats += [jnp.sum(scaled * kept[m], axis=-1) for m in range(extent - 1)]
            stats += [jnp.sum(scaled * scaled, axis=-1), jnp.sum(scaled * mixed, axis=-1)]
            stats += [jnp.sum(mixed * kept[m], axis=-1) for m in range(extent - 1)]
            stats += [jnp.sum(mixed * mixed, axis=-1)]
            received = exchange(jnp.stack(stats), ("seq", "tp"))
            sums = jnp.sum(received.reshape((seq_count, tp_count) + received.shape[1:]), axis=1)
            row_scale = lax.rsqrt(sums[:, 0] / full_width + epsilon)
            cross = sums[:, 1:extent] * row_scale[:, None] - sums[:, extent + 2:2 * extent + 1]
            cross = jnp.sum(cross, axis=0)
            own_terms = jnp.sum(
                row_scale * row_scale * sums[:, extent]
                - 2.0 * row_scale * sums[:, extent + 1]
                + sums[:, 2 * extent + 1],
                axis=0,
            )
            fresh = []
            for m, n in pairs:
                if n < extent - 1:
                    fresh.append(gram_rows[pairs.index((m + 1, n + 1))])
                elif m < extent - 1:
                    fresh.append(cross[m])
                else:
                    fresh.append(own_terms)
            gram_rows = jnp.stack(fresh)
            own_scale = lax.dynamic_index_in_dim(row_scale, seq_index, 0, keepdims=False)
            image = scaled * own_scale[:, None]
            kept = jnp.concatenate([kept, (image - mixed)[None]], axis=0)
            images = jnp.concatenate([images[1:], image[None]], axis=0)
    return (mixed[None], image[None])


def solution(mesh):
    in_specs = (
        P(None, "seq", "tp"),
        P(None, None, "tp"),
        P("tp", None),
        P("tp"),
        P("tp"),
        P(None, None, "seq", "tp"),
        P(None, None, "seq", "tp"),
    )
    out_specs = (P(None, "seq", "tp"), P(None, "seq", "tp"))
    return jax.shard_map(shards, mesh=mesh, in_specs=in_specs, out_specs=out_specs, check_vma=False)
```
